128 devices in a mesh: wide: 32 (over z, y, core), narrow: 4 (over x).
Axes of the slice: x: 4, y: 4, z: 4, core: 2. Of those that a mesh axis runs over, the one named last changes fastest.
Arguments:
- slab: float32 [4, 512, 512, 256], P(None, 'narrow', 'wide'), may hold values from -180 to 180
- factor: float32 [512, 64], replicated, may hold values from -0.25 to 0.25
Outputs:
- r_factor: float32 [512, 512], replicated
- core: float32 [4, 64, 512, 256], P(None, None, 'wide', 'narrow')
The draws below stay inside these ranges and needn't reach their ends.
All inputs are finite; a program needn't handle non-finite values.
Results may differ from the reference program's by a relative error of at most 0.00007.
Values sent between devices are 32-bit elements; how exact they have to be, the bound alone decides.
No kernel may reach another device: no remote copies, remote signals or barrier semaphores. Data moves between devices by JAX's collectives and lax.ppermute only.
A program may use at most 256 MiB of HBM per device.

```python
import math
import jax
import jax.numpy as jnp
from jax import lax

D1 = 512
RANK = 64
COMP = 4
I3 = 256
I2 = 512
NCOL = 524288


def draw_slab(key, part):
    keys = jax.random.split(key, 5)
    shape = (COMP, D1, I2, I3)
    noise = jnp.clip(jax.random.normal(keys[0], shape, jnp.float32), -6.0, 6.0)
    before = jnp.roll(noise, 1, axis=1)
    lean = jax.random.uniform(keys[1], (1, D1, 1, 1), jnp.float32, 0.3, 0.8)
    scale = jnp.exp(jax.random.uniform(keys[2], (1, D1, 1, 1), jnp.float32, math.log(0.5), math.log(5.0)))
    share = jax.random.uniform(keys[3], (1, D1, 1, 1), jnp.float32, -1.0, 1.0)
    rise = 1.0 + 2.0 * jnp.arange(I2, dtype=jnp.float32).reshape(1, 1, I2, 1) / max(I2 - 1, 1)
    common = jnp.clip(jax.random.normal(keys[4], (COMP, 1, I2, I3), jnp.float32), -6.0, 6.0)
    value = rise * (scale * (noise + lean * before) + share * common)
    return value.astype(jnp.float32)


def gaussian(stream_key, shape, deviation, limit, kind=jnp.bfloat16):
    return jnp.clip(deviation * jax.random.normal(stream_key, shape, jnp.float32), -limit, limit).astype(kind)


def setup_inputs(seed: int = 0) -> dict:
    streams_of = jax.random.split(jax.random.key(seed), 3)
    slab = draw_slab(jax.random.fold_in(streams_of[2], 71), 0)
    factor = gaussian(streams_of[1], (D1, RANK), D1 ** -0.5, 0.25, jnp.float32)
    return dict(slab=slab, factor=factor)


def reference(slab, factor):

    def one_comp(block):
        return jnp.einsum('iab,jab->ij', block, block, precision=lax.Precision.HIGHEST)
    grams = lax.map(one_comp, slab)
    gram = jnp.sum(grams, axis=0) / NCOL
    r_factor = jnp.linalg.cholesky(gram).T
    core = jnp.einsum('ir,ciab->crab', factor, slab, precision=lax.Precision.HIGHEST)
    return (r_factor, core)
```

```python
import functools
import jax
import jax.numpy as jnp
from jax import lax
from jax.experimental import pallas as pl
from jax.experimental.pallas import tpu as pltpu
from jax.sharding import PartitionSpec as P

HI = lax.Precision.HIGHEST
BLOCKS = [(i, j) for i in range(4) for j in range(i, 4)]
SHIFTS = (1, 3, 2)


def ring(axis_size, step, stride, shift):
    span = step * stride
    return [
        (i, i - (i % span) + ((i % span) + shift * stride) % span)
        for i in range(axis_size)
    ]


def pack_kernel(x0_ref, x1_ref, *outs):
    n = lax.axis_index("narrow")
    rows = x0_ref.shape[0] // 16
    low = lax.broadcasted_iota(jnp.int32, (rows, 128), 1) < 64

    def body(k):
        for a in range(8):
            for tile, x_ref in enumerate((x0_ref, x1_ref)):
                lo = x_ref[pl.ds(a, rows, stride=16), :]
                hi = x_ref[pl.ds(a + 8, rows, stride=16), :]
                even = jnp.where(low, lo, pltpu.roll(hi, 64, 1))
                odd = jnp.where(low, pltpu.roll(lo, 64, 1), hi)
                outs[(2 * tile - k) % 4][a] = even
                outs[(2 * tile + 1 - k) % 4][a] = odd

    for k in range(4):
        pl.when(n == k)(functools.partial(body, k))


def pack(slab, comp):
    rows = 512
    return pl.pallas_call(
        pack_kernel,
        grid=(4,),
        in_specs=[
            pl.BlockSpec((None, rows, 128), lambda i: (comp, i, 0)),
            pl.BlockSpec((None, rows, 128), lambda i: (comp, i, 1)),
        ],
        out_specs=[pl.BlockSpec((8, rows // 16, 128), lambda i: (0, i, 0))] * 4,
        out_shape=[jax.ShapeDtypeStruct((8, 128, 128), jnp.float32)] * 4,
        cost_estimate=pl.CostEstimate(
            flops=1 << 20, bytes_accessed=4 << 20, transcendentals=0
        ),
        name="pack",
    )(slab, slab)


def gram_kernel(first, *refs):
    if first:
        own, r1, r3, r2, factor_ref, acc_ref, core_ref, x_scr, core_scr = refs
    else:
        own, r1, r3, r2, factor_ref, acc_in, _, acc_ref, core_ref, x_scr, core_scr = refs
    m = lax.axis_index("narrow")
    step = pl.program_id(0)
    for shift, piece in ((0, own), (1, r1), (3, r3), (2, r2)):
        row = pl.multiple_of(lax.rem(m + 4 - shift, 4) * 128, 128)
        for a in range(2):
            x_scr[pl.ds(row, 128), a * 128:(a + 1) * 128] = piece[a]

    @pl.when(step == 0)
    def _():
        if first:
            acc_ref[...] = jnp.zeros_like(acc_ref)
        else:
            acc_ref[...] = acc_in[...]

    x = x_scr[...]
    block = 0
    for i in range(4):
        part = lax.dot_general(
            x[i * 128:(i + 1) * 128],
            x[i * 128:],
            (((1,), (1,)), ((), ())),
            precision=HI,
            preferred_element_type=jnp.float32,
        )
        for j in range(4 - i):
            acc_ref[block * 128:(block + 1) * 128, :] += part[:, j * 128:(j + 1) * 128]
            block += 1
    core = jnp.dot(factor_ref[...], x, precision=HI, preferred_element_type=jnp.float32)
    for a in range(2):
        part = core[:, a * 128:(a + 1) * 128]
        at = 2 * step + a
        core_scr[pl.ds(at, 64, stride=16), :] = part
        core_scr[pl.ds(at + 8, 64, stride=16), :] = pltpu.roll(part, 64, 1)

    @pl.when(step == pl.num_programs(0) - 1)
    def _():
        core_ref[...] = core_scr[:, :64]


def gram_step(comp, pieces, factor_t, acc, core):
    first = acc is None
    piece_spec = pl.BlockSpec((2, 128, 128), lambda s: (s, 0, 0))
    in_specs = [piece_spec] * 4 + [pl.BlockSpec((64, 512), lambda s: (0, 0))]
    args = list(pieces) + [factor_t]
    aliases = {}
    if not first:
        in_specs += [
            pl.BlockSpec((1280, 128), lambda s: (0, 0)),
            pl.BlockSpec(memory_space=pl.ANY),
        ]
        args += [acc, core]
        aliases = {5: 0, 6: 1}
    return pl.pallas_call(
        functools.partial(gram_kernel, first),
        grid=(4,),
        in_specs=in_specs,
        out_specs=[
            pl.BlockSpec((1280, 128), lambda s: (0, 0)),
            pl.BlockSpec((None, 1024, 64), lambda s: (comp, 0, 0)),
        ],
        out_shape=[
            jax.ShapeDtypeStruct((1280, 128), jnp.float32),
            jax.ShapeDtypeStruct((4, 1024, 64), jnp.float32),
        ],
        scratch_shapes=[
            pltpu.VMEM((512, 256), jnp.float32),
            pltpu.VMEM((1024, 128), jnp.float32),
        ],
        input_output_aliases=aliases,
        cost_estimate=pl.CostEstimate(
            flops=6 << 29, bytes_accessed=4 << 20, transcendentals=0
        ),
        name="gram",
    )(*args)


def exchange(parts, axis, step, stride):
    size = lax.axis_size(axis)
    return [
        lax.ppermute(p, axis, ring(size, step, stride, k))
        for k, p in zip(SHIFTS, parts)
    ]


def scatter_sum(x, axis, pos, stride):
    rows = x.shape[0] // 4
    pick = lambda at: lax.dynamic_slice_in_dim(x, at * rows, rows)
    got = exchange([pick((pos + k) % 4) for k in SHIFTS], axis, 4, stride)
    return pick(pos) + got[0] + got[1] + got[2]


def gather(x, axis, pos, stride):
    got = exchange([x] * 3, axis, 4, stride)
    rows = x.shape[0]
    out = jnp.zeros((4 * rows,) + x.shape[1:], x.dtype)
    out = lax.dynamic_update_slice_in_dim(out, x, pos * rows, 0)
    for k, g in zip(SHIFTS, got):
        out = lax.dynamic_update_slice_in_dim(out, g, ((pos + 4 - k) % 4) * rows, 0)
    return out


def total(acc):
    wide = lax.axis_index("wide")
    nx = lax.axis_index("narrow")
    core, ny, nz = wide % 2, (wide // 2) % 4, wide // 8
    swap = ring(lax.axis_size("wide"), 2, 1, 1)
    half = acc.shape[0] // 2
    mine = lax.dynamic_slice_in_dim(acc, core * half, half)
    give = lax.dynamic_slice_in_dim(acc, (1 - core) * half, half)
    h = mine + lax.ppermute(give, "wide", swap)
    h = scatter_sum(h, "narrow", nx, 1)
    h = scatter_sum(h, "wide", ny, 2)
    got = exchange([h] * 3, "wide", 4, 8)
    parts = [h] + got
    order = [parts[0], parts[1], parts[3], parts[2]]
    stack = jnp.stack(order)
    turn = lambda z: lax.dynamic_index_in_dim(stack, (nz + 4 - z) % 4, 0, keepdims=False)
    h = ((turn(0) + turn(1)) + turn(2)) + turn(3)
    h = gather(h, "wide", ny, 2)
    h = gather(h, "narrow", nx, 1)
    o = lax.ppermute(h, "wide", swap)
    return jnp.where(core == 0, jnp.concatenate([h, o]), jnp.concatenate([o, h]))


def on_device(slab, factor):
    count, own, second, third = slab.shape
    ncol_total = count * second * lax.axis_size("wide") * third
    flat = slab.reshape(count, own * second, third)
    factor_t = factor.T
    acc = core = None
    packed = [pack(flat, c) for c in range(count)]
    for c in range(count):
        p = packed[c]
        got = [
            lax.ppermute(p[k], "narrow", ring(4, 4, 1, k)) for k in SHIFTS
        ]
        acc, core = gram_step(c, [p[0]] + got, factor_t, acc, core)
    blocks = (total(acc) / ncol_total).reshape(10, 128, 128)
    rows = []
    at = {b: k for k, b in enumerate(BLOCKS)}
    for i in range(4):
        row = []
        for j in range(4):
            row.append(blocks[at[(i, j)]] if i <= j else blocks[at[(j, i)]].T)
        rows.append(jnp.concatenate(row, axis=1))
    gram = jnp.concatenate(rows, axis=0)
    r_factor = jnp.linalg.cholesky(gram).T
    return (r_factor, core.reshape(count, 64, second, 64))


def solution(mesh):
    return jax.shard_map(
        on_device,
        mesh=mesh,
        in_specs=(P(None, "narrow", "wide", None), P()),
        out_specs=(P(), P(None, None, "wide", "narrow")),
        check_vma=False,
    )
```

```python
import functools
import jax
import jax.numpy as jnp
from jax import lax
from jax.experimental import pallas as pl
from jax.experimental.pallas import tpu as pltpu
from jax.sharding import Mesh, PartitionSpec as P

HI = lax.Precision.HIGHEST
BLOCKS = [(i, j) for i in range(4) for j in range(i, 4)]
SHIFTS = (1, 3, 2)
HALF = 640
PAD = 1024
F32 = jnp.float32
BF16 = jnp.bfloat16


def ring(size, shift):
    return [(i, (i + shift) % size) for i in range(size)]


def pack_kernel(x0_ref, x1_ref, *outs):
    n = lax.axis_index("narrow")
    rows = x0_ref.shape[0] // 16
    parts = len(outs) // 4
    depth = 8 // parts
    low = lax.broadcasted_iota(jnp.int32, (rows, 128), 1) < 64

    def body(k):
        for a in range(8):
            for tile, x_ref in enumerate((x0_ref, x1_ref)):
                lo = x_ref[pl.ds(a, rows, stride=16), :]
                hi = x_ref[pl.ds(a + 8, rows, stride=16), :]
                even = jnp.where(low, lo, pltpu.roll(hi, 64, 1))
                odd = jnp.where(low, pltpu.roll(lo, 64, 1), hi)
                base = 4 * (a // depth)
                outs[base + (2 * tile - k) % 4][a % depth] = even
                outs[base + (2 * tile + 1 - k) % 4][a % depth] = odd

    for k in range(4):
        pl.when(n == k)(functools.partial(body, k))


def pack(slab, comp, parts):
    rows = 512
    depth = 8 // parts
    outs = pl.pallas_call(
        pack_kernel,
        grid=(4,),
        in_specs=[
            pl.BlockSpec((None, rows, 128), lambda i: (comp, i, 0)),
            pl.BlockSpec((None, rows, 128), lambda i: (comp, i, 1)),
        ],
        out_specs=[pl.BlockSpec((depth, rows // 16, 128), lambda i: (0, i, 0))] * (4 * parts),
        out_shape=[jax.ShapeDtypeStruct((depth, 128, 128), F32)] * (4 * parts),
        cost_estimate=pl.CostEstimate(
            flops=1 << 20, bytes_accessed=4 << 20, transcendentals=0
        ),
        name="pack",
    )(slab, slab)
    return [outs[4 * k:4 * k + 4] for k in range(parts)]


def split(x):
    h = x.astype(BF16)
    rest = x - h.astype(F32)
    m = rest.astype(BF16)
    l = (rest - m.astype(F32)).astype(BF16)
    return h, m, l


def nt(a, b):
    return lax.dot_general(a, b, (((1,), (1,)), ((), ())), preferred_element_type=F32)


def gram_kernel(first, last, merge, base, *refs):
    own, r1, r3, r2, factor_ref = refs[:5]
    refs = refs[5:]
    acc_in = None
    if not first:
        acc_in, core_in = refs[:2]
        refs = refs[2:]
    if last:
        mine_ref, give_ref, core_ref, h_scr, m_scr, l_scr, core_scr, acc_ref = refs
    else:
        acc_ref, core_ref, h_scr, m_scr, l_scr, core_scr = refs
    me = lax.axis_index("narrow")
    step = pl.program_id(0)
    for shift, piece in ((0, own), (1, r1), (3, r3), (2, r2)):
        row = pl.multiple_of(lax.rem(me + 4 - shift, 4) * 128, 128)
        for a in range(4):
            h, m, l = split(piece[a])
            lanes = slice(a * 128, (a + 1) * 128)
            h_scr[pl.ds(row, 128), lanes] = h
            m_scr[pl.ds(row, 128), lanes] = m
            l_scr[pl.ds(row, 128), lanes] = l

    @pl.when(step == 0)
    def _():
        if first:
            acc_ref[...] = jnp.zeros_like(acc_ref)
        else:
            acc_ref[...] = acc_in[...]
        if merge:
            core_scr[:, :64] = core_in[...]

    for top, side in ((256, 0), (512, 256)):
        a = [s[:top, :] for s in (h_scr, m_scr, l_scr)]
        b = [s[side:side + 256, :] for s in (h_scr, m_scr, l_scr)]
        part = nt(a[1], b[1])
        part += nt(a[0], b[2])
        part += nt(a[2], b[0])
        part += nt(a[0], b[1])
        part += nt(a[1], b[0])
        part += nt(a[0], b[0])
        for k, (i, j) in enumerate(BLOCKS):
            if side <= j * 128 < side + 256:
                acc_ref[k * 128:(k + 1) * 128, :] += part[
                    i * 128:(i + 1) * 128, j * 128 - side:j * 128 - side + 128
                ]
    f = jnp.concatenate(split(factor_ref[...]), axis=0)
    by_h = jnp.dot(f, h_scr[...], preferred_element_type=F32)
    by_m = jnp.dot(f[:128], m_scr[...], preferred_element_type=F32)
    by_l = jnp.dot(f[:64], l_scr[...], preferred_element_type=F32)
    core = (by_h[128:] + by_l + by_m[64:]) + (by_h[64:128] + by_m[:64]) + by_h[:64]
    for a in range(4):
        part = core[:, a * 128:(a + 1) * 128]
        at = base + 4 * step + a
        core_scr[pl.ds(at, 64, stride=16), :] = part
        core_scr[pl.ds(at + 8, 64, stride=16), :] = pltpu.roll(part, 64, 1)

    @pl.when(step == pl.num_programs(0) - 1)
    def _():
        core_ref[...] = core_scr[:, :64]
        if last:
            c = lax.axis_index("core")
            mine_ref[...] = acc_ref[pl.ds(pl.multiple_of(c * HALF, 128), HALF), :]
            give_ref[...] = acc_ref[pl.ds(pl.multiple_of((1 - c) * HALF, 128), HALF), :]


def gram_step(comp, base, pieces, factor_t, acc, core, last):
    first = acc is None
    merge = base > 0
    depth = pieces[0].shape[0]
    piece_spec = pl.BlockSpec((4, 128, 128), lambda s: (s, 0, 0))
    whole = lambda s: (0, 0)
    in_specs = [piece_spec] * 4 + [pl.BlockSpec((64, 512), whole)]
    core_spec = pl.BlockSpec((None, 1024, 64), lambda s: (comp, 0, 0))
    args = list(pieces) + [factor_t]
    aliases = {}
    if not first:
        in_specs += [
            pl.BlockSpec((1280, 128), whole),
            core_spec if merge else pl.BlockSpec(memory_space=pl.ANY),
        ]
        args += [acc, core]
        aliases = {6: 2} if last else {5: 0, 6: 1}
    sums = [HALF, HALF] if last else [1280]
    scratch = [pltpu.VMEM((512, 512), BF16)] * 3 + [pltpu.VMEM((1024, 128), F32)]
    if last:
        scratch.append(pltpu.VMEM((1280, 128), F32))
    return pl.pallas_call(
        functools.partial(gram_kernel, first, last, merge, base),
        grid=(depth // 4,),
        in_specs=in_specs,
        out_specs=[pl.BlockSpec((r, 128), whole) for r in sums] + [core_spec],
        out_shape=[jax.ShapeDtypeStruct((r, 128), F32) for r in sums]
        + [jax.ShapeDtypeStruct((4, 1024, 64), F32)],
        scratch_shapes=scratch,
        input_output_aliases=aliases,
        compiler_params=pltpu.CompilerParams(vmem_limit_bytes=40 << 20),
        cost_estimate=pl.CostEstimate(
            flops=(6 << 26) * depth, bytes_accessed=depth << 19, transcendentals=0
        ),
        name="gram",
    )(*args)


def total(mine, give):
    swap = [(0, 1), (1, 0)]
    count = lax.axis_size("chip") * lax.axis_size("narrow")
    h = mine + lax.ppermute(give, "core", swap)
    h = jnp.pad(h, ((0, PAD - HALF), (0, 0))).reshape(count, PAD // count, 128)
    h = deal(h)
    piece = jnp.sum(h, axis=0)
    h = deal(jnp.broadcast_to(piece[None], h.shape))
    h = h.reshape(PAD, 128)[:HALF]
    return h, lax.ppermute(h, "core", swap)


def deal(x):
    return lax.all_to_all(x, ("chip", "narrow"), 0, 0, tiled=True)


def factor_block(work, out_ref, b, tiles):
    lane = lax.broadcasted_iota(jnp.int32, (8, 128), 1)
    sub = lax.broadcasted_iota(jnp.int32, (8, 128), 0)
    base = b * 128
    spread = lambda v, i: jnp.broadcast_to(v[i:i + 1, :], (8, 128))
    column = lambda v, j: jnp.broadcast_to(v[:, j:j + 1], (8, 128))
    for p in range(16):
        at = base + 8 * p
        head = work[b, at:at + 8, :]
        cols = [column(head, 8 * p + j) for j in range(8)]
        c = {(i, j): spread(cols[j], i) for j in range(8) for i in range(j + 1)}
        rs, u = [], {}
        for k in range(8):
            r = lax.rsqrt(c[k, k])
            rs.append(r)
            for j in range(k + 1, 8):
                u[k, j] = c[k, j] * r
            for j in range(k + 1, 8):
                for i in range(k + 1, j + 1):
                    c[i, j] = c[i, j] - u[k, i] * u[k, j]
        rows = {}
        for t in tiles:
            x = head if t == b else work[t, at:at + 8, :]
            made = []
            for k in range(8):
                v = spread(x, k)
                for m in range(k):
                    v = v - u[m, k] * made[m]
                made.append(v * rs[k])
            rows[t] = made
            full = made[0]
            for k in range(1, 8):
                full = jnp.where(sub >= k, made[k], full)
            if t == b:
                full = jnp.where(lane >= sub + 8 * p, full, 0.0)
            out_ref[at:at + 8, t * 128:(t + 1) * 128] = full
        for g in range(p + 1, 16):
            ag = base + 8 * g
            a = work[b, ag:ag + 8, :]
            left = [column(a, 8 * p + j) for j in range(8)]
            ug = []
            for k in range(8):
                w = left[k] * rs[k]
                ug.append(w)
                for j in range(k + 1, 8):
                    left[j] = left[j] - w * u[k, j]
            for t in tiles:
                v = a if t == b else work[t, ag:ag + 8, :]
                for k in range(8):
                    v = v - ug[k] * rows[t][k]
                work[t, ag:ag + 8, :] = v


def chol_kernel(scale, mine_ref, other_ref, out_ref, gram, work):
    c = lax.axis_index("core")
    gram[pl.ds(pl.multiple_of(c * HALF, 128), HALF), :] = mine_ref[...]
    gram[pl.ds(pl.multiple_of((1 - c) * HALF, 128), HALF), :] = other_ref[...]
    for k, (i, j) in enumerate(BLOCKS):
        work[j, i * 128:(i + 1) * 128, :] = gram[k * 128:(k + 1) * 128, :] * scale
    for b in range(4):
        factor_block(work, out_ref, b, range(b, 4))
        for t in range(b):
            out_ref[b * 128:(b + 1) * 128, t * 128:(t + 1) * 128] = jnp.zeros((128, 128), F32)
        if b < 3:
            tail = out_ref[b * 128:(b + 1) * 128, (b + 1) * 128:]
            for i in range(b + 1, 4):
                o = (i - b - 1) * 128
                part = lax.dot_general(
                    tail[:, o:o + 128],
                    tail[:, o:],
                    (((0,), (0,)), ((), ())),
                    precision=HI,
                    preferred_element_type=F32,
                )
                for j in range(i, 4):
                    work[j, i * 128:(i + 1) * 128, :] -= part[:, (j - i) * 128:(j - i + 1) * 128]


def upper_factor(mine, other, scale):
    return pl.pallas_call(
        functools.partial(chol_kernel, scale),
        out_shape=jax.ShapeDtypeStruct((512, 512), F32),
        in_specs=[pl.BlockSpec((HALF, 128), lambda: (0, 0))] * 2,
        out_specs=pl.BlockSpec((512, 512), lambda: (0, 0)),
        scratch_shapes=[pltpu.VMEM((1280, 128), F32), pltpu.VMEM((4, 512, 128), F32)],
        name="upper_factor",
    )(mine, other)


def on_device(slab, factor):
    count, own, second, third = slab.shape
    ncol_total = count * second * lax.axis_size("chip") * lax.axis_size("core") * third
    flat = slab.reshape(count, own * second, third)
    factor_t = factor.T
    acc = core = None
    chunks = []
    for c in range(count):
        parts = 2 if c == count - 1 else 1
        for k, p in enumerate(pack(flat, c, parts)):
            chunks.append((c, k * (8 // parts), p))
    for at, (c, base, p) in enumerate(chunks):
        got = [lax.ppermute(p[k], "narrow", ring(4, k)) for k in SHIFTS]
        last = at == len(chunks) - 1
        made = gram_step(c, base, [p[0]] + got, factor_t, acc, core, last)
        if last:
            mine, give, core = made
        else:
            acc, core = made
    mine, other = total(mine, give)
    r_factor = upper_factor(mine, other, 1.0 / ncol_total)
    return (r_factor, core.reshape(count, 64, second, 64))


def solution(mesh):
    wide, narrow = mesh.devices.shape
    split_mesh = Mesh(
        mesh.devices.reshape(wide // 2, 2, narrow), ("chip", "core", "narrow")
    )
    return jax.shard_map(
        on_device,
        mesh=split_mesh,
        in_specs=(P(None, "narrow", ("chip", "core"), None), P()),
        out_specs=(P(), P(None, None, ("chip", "core"), "narrow")),
        check_vma=False,
    )
```

```python
import functools
import jax
import jax.numpy as jnp
from jax import lax
from jax.experimental import pallas as pl
from jax.experimental.pallas import tpu as pltpu
from jax.sharding import Mesh, PartitionSpec as P

HI = lax.Precision.HIGHEST
BLOCKS = [(i, j) for i in range(4) for j in range(i, 4)]
SHIFTS = (1, 3, 2)
HALF = 640
WIDE = ("z", "y", "core")
F32 = jnp.float32
BF16 = jnp.bfloat16


def ring(size, shift):
    return [(i, (i + shift) % size) for i in range(size)]


def pack_kernel(x0_ref, x1_ref, *outs):
    n = lax.axis_index("narrow")
    rows = x0_ref.shape[0] // 16
    parts = len(outs) // 4
    depth = 8 // parts
    low = lax.broadcasted_iota(jnp.int32, (rows, 128), 1) < 64

    def body(k):
        for part in range(parts):

            @pl.loop(0, depth)
            def _(a):
                at = part * depth + a
                for tile, x_ref in enumerate((x0_ref, x1_ref)):
                    lo = x_ref[pl.ds(at, rows, stride=16), :]
                    hi = x_ref[pl.ds(at + 8, rows, stride=16), :]
                    even = jnp.where(low, lo, pltpu.roll(hi, 64, 1))
                    odd = jnp.where(low, pltpu.roll(lo, 64, 1), hi)
                    outs[4 * part + (2 * tile - k) % 4][a] = even
                    outs[4 * part + (2 * tile + 1 - k) % 4][a] = odd

    for k in range(4):
        pl.when(n == k)(functools.partial(body, k))


def pack(slab, comp, parts):
    rows = 1024
    depth = 8 // parts
    outs = pl.pallas_call(
        pack_kernel,
        grid=(2,),
        in_specs=[
            pl.BlockSpec((None, rows, 128), lambda i: (comp, i, 0)),
            pl.BlockSpec((None, rows, 128), lambda i: (comp, i, 1)),
        ],
        out_specs=[pl.BlockSpec((depth, rows // 16, 128), lambda i: (0, i, 0))] * (4 * parts),
        out_shape=[jax.ShapeDtypeStruct((depth, 128, 128), F32)] * (4 * parts),
        cost_estimate=pl.CostEstimate(
            flops=1 << 20, bytes_accessed=4 << 20, transcendentals=0
        ),
        name="pack",
    )(slab, slab)
    return [outs[4 * k:4 * k + 4] for k in range(parts)]


def split(x):
    h = x.astype(BF16)
    rest = x - h.astype(F32)
    m = rest.astype(BF16)
    l = (rest - m.astype(F32)).astype(BF16)
    return h, m, l


def nt(a, b):
    return lax.dot_general(a, b, (((1,), (1,)), ((), ())), preferred_element_type=F32)


def gram_kernel(first, last, merge, base, *refs):
    own, r1, r3, r2, factor_ref = refs[:5]
    refs = refs[5:]
    acc_in = None
    if not first:
        acc_in, core_in = refs[:2]
        refs = refs[2:]
    if last:
        mine_ref, give_ref, core_ref, h_scr, m_scr, l_scr, core_scr, acc_ref = refs
    else:
        acc_ref, core_ref, h_scr, m_scr, l_scr, core_scr = refs
    me = lax.axis_index("narrow")
    step = pl.program_id(0)
    for shift, piece in ((0, own), (1, r1), (3, r3), (2, r2)):
        row = pl.multiple_of(lax.rem(me + 4 - shift, 4) * 128, 128)
        for a in range(4):
            h, m, l = split(piece[a])
            lanes = slice(a * 128, (a + 1) * 128)
            h_scr[pl.ds(row, 128), lanes] = h
            m_scr[pl.ds(row, 128), lanes] = m
            l_scr[pl.ds(row, 128), lanes] = l

    @pl.when(step == 0)
    def _():
        if first:
            acc_ref[...] = jnp.zeros_like(acc_ref)
        else:
            acc_ref[...] = acc_in[...]
        if merge:
            core_scr[:, :64] = core_in[...]

    for top, side in ((256, 0), (512, 256)):
        a = [s[:top, :] for s in (h_scr, m_scr, l_scr)]
        b = [s[side:side + 256, :] for s in (h_scr, m_scr, l_scr)]
        part = nt(a[1], b[1])
        part += nt(a[0], b[2])
        part += nt(a[2], b[0])
        part += nt(a[0], b[1])
        part += nt(a[1], b[0])
        part += nt(a[0], b[0])
        for k, (i, j) in enumerate(BLOCKS):
            if side <= j * 128 < side + 256:
                acc_ref[k * 128:(k + 1) * 128, :] += part[
                    i * 128:(i + 1) * 128, j * 128 - side:j * 128 - side + 128
                ]
    f = jnp.concatenate(split(factor_ref[...]), axis=0)
    by_h = jnp.dot(f, h_scr[...], preferred_element_type=F32)
    by_m = jnp.dot(f[:128], m_scr[...], preferred_element_type=F32)
    by_l = jnp.dot(f[:64], l_scr[...], preferred_element_type=F32)
    core = (by_h[128:] + by_l + by_m[64:]) + (by_h[64:128] + by_m[:64]) + by_h[:64]
    for a in range(4):
        part = core[:, a * 128:(a + 1) * 128]
        at = base + 4 * step + a
        core_scr[pl.ds(at, 64, stride=16), :] = part
        core_scr[pl.ds(at + 8, 64, stride=16), :] = pltpu.roll(part, 64, 1)

    @pl.when(step == pl.num_programs(0) - 1)
    def _():
        core_ref[...] = core_scr[:, :64]
        if last:
            c = lax.axis_index("core")
            mine_ref[...] = acc_ref[pl.ds(pl.multiple_of(c * HALF, 128), HALF), :]
            give_ref[...] = acc_ref[pl.ds(pl.multiple_of((1 - c) * HALF, 128), HALF), :]


def gram_step(comp, base, pieces, factor_t, acc, core, last):
    first = acc is None
    merge = base > 0
    depth = pieces[0].shape[0]
    piece_spec = pl.BlockSpec((4, 128, 128), lambda s: (s, 0, 0))
    whole = lambda s: (0, 0)
    in_specs = [piece_spec] * 4 + [pl.BlockSpec((64, 512), whole)]
    core_spec = pl.BlockSpec((None, 1024, 64), lambda s: (comp, 0, 0))
    args = list(pieces) + [factor_t]
    aliases = {}
    if not first:
        in_specs += [
            pl.BlockSpec((1280, 128), whole),
            core_spec if merge else pl.BlockSpec(memory_space=pl.ANY),
        ]
        args += [acc, core]
        aliases = {6: 2} if last else {5: 0, 6: 1}
    sums = [HALF, HALF] if last else [1280]
    scratch = [pltpu.VMEM((512, 512), BF16)] * 3 + [pltpu.VMEM((1024, 128), F32)]
    if last:
        scratch.append(pltpu.VMEM((1280, 128), F32))
    return pl.pallas_call(
        functools.partial(gram_kernel, first, last, merge, base),
        grid=(depth // 4,),
        in_specs=in_specs,
        out_specs=[pl.BlockSpec((r, 128), whole) for r in sums] + [core_spec],
        out_shape=[jax.ShapeDtypeStruct((r, 128), F32) for r in sums]
        + [jax.ShapeDtypeStruct((4, 1024, 64), F32)],
        scratch_shapes=scratch,
        input_output_aliases=aliases,
        compiler_params=pltpu.CompilerParams(vmem_limit_bytes=40 << 20),
        cost_estimate=pl.CostEstimate(
            flops=(6 << 26) * depth, bytes_accessed=depth << 19, transcendentals=0
        ),
        name="gram",
    )(*args)


def total(mine, give):
    swap = [(0, 1), (1, 0)]
    plane = lax.axis_size("z") * lax.axis_size("y")
    h = mine + lax.ppermute(give, "core", swap)
    h = h.reshape(plane, HALF // plane, 128)
    deal = lambda x, axes: lax.all_to_all(x, axes, 0, 0, tiled=True)
    spread = lambda x, n: jnp.broadcast_to(x[None], (n,) + x.shape)
    piece = jnp.sum(deal(h, ("z", "y")), axis=0)
    piece = jnp.sum(deal(spread(piece, lax.axis_size("narrow")), "narrow"), axis=0)
    h = deal(spread(piece, plane), ("z", "y")).reshape(HALF, 128)
    return h, lax.ppermute(h, "core", swap)


def factor_block(work, out_ref, b, tiles):
    lane = lax.broadcasted_iota(jnp.int32, (8, 128), 1)
    sub = lax.broadcasted_iota(jnp.int32, (8, 128), 0)
    base = b * 128
    spread = lambda v, i: jnp.broadcast_to(v[i:i + 1, :], (8, 128))
    column = lambda v, j: jnp.broadcast_to(v[:, j:j + 1], (8, 128))
    for p in range(16):
        at = base + 8 * p
        head = work[b, at:at + 8, :]
        cols = [column(head, 8 * p + j) for j in range(8)]
        c = {(i, j): spread(cols[j], i) for j in range(8) for i in range(j + 1)}
        rs, u = [], {}
        for k in range(8):
            r = lax.rsqrt(c[k, k])
            rs.append(r)
            for j in range(k + 1, 8):
                u[k, j] = c[k, j] * r
            for j in range(k + 1, 8):
                for i in range(k + 1, j + 1):
                    c[i, j] = c[i, j] - u[k, i] * u[k, j]
        rows = {}
        for t in tiles:
            x = head if t == b else work[t, at:at + 8, :]
            made = []
            for k in range(8):
                v = spread(x, k)
                for m in range(k):
                    v = v - u[m, k] * made[m]
                made.append(v * rs[k])
            rows[t] = made
            full = made[0]
            for k in range(1, 8):
                full = jnp.where(sub >= k, made[k], full)
            if t == b:
                full = jnp.where(lane >= sub + 8 * p, full, 0.0)
            out_ref[at:at + 8, t * 128:(t + 1) * 128] = full
        for g in range(p + 1, 16):
            ag = base + 8 * g
            a = work[b, ag:ag + 8, :]
            left = [column(a, 8 * p + j) for j in range(8)]
            ug = []
            for k in range(8):
                w = left[k] * rs[k]
                ug.append(w)
                for j in range(k + 1, 8):
                    left[j] = left[j] - w * u[k, j]
            for t in tiles:
                v = a if t == b else work[t, ag:ag + 8, :]
                for k in range(8):
                    v = v - ug[k] * rows[t][k]
                work[t, ag:ag + 8, :] = v


def chol_kernel(scale, mine_ref, other_ref, out_ref, gram, work):
    c = lax.axis_index("core")
    gram[pl.ds(pl.multiple_of(c * HALF, 128), HALF), :] = mine_ref[...]
    gram[pl.ds(pl.multiple_of((1 - c) * HALF, 128), HALF), :] = other_ref[...]
    for k, (i, j) in enumerate(BLOCKS):
        work[j, i * 128:(i + 1) * 128, :] = gram[k * 128:(k + 1) * 128, :] * scale
    for b in range(4):
        factor_block(work, out_ref, b, range(b, 4))
        for t in range(b):
            out_ref[b * 128:(b + 1) * 128, t * 128:(t + 1) * 128] = jnp.zeros((128, 128), F32)
        if b < 3:
            tail = out_ref[b * 128:(b + 1) * 128, (b + 1) * 128:]
            for i in range(b + 1, 4):
                o = (i - b - 1) * 128
                part = lax.dot_general(
                    tail[:, o:o + 128],
                    tail[:, o:],
                    (((0,), (0,)), ((), ())),
                    precision=HI,
                    preferred_element_type=F32,
                )
                for j in range(i, 4):
                    work[j, i * 128:(i + 1) * 128, :] -= part[:, (j - i) * 128:(j - i + 1) * 128]


def upper_factor(mine, other, scale):
    return pl.pallas_call(
        functools.partial(chol_kernel, scale),
        out_shape=jax.ShapeDtypeStruct((512, 512), F32),
        in_specs=[pl.BlockSpec((HALF, 128), lambda: (0, 0))] * 2,
        out_specs=pl.BlockSpec((512, 512), lambda: (0, 0)),
        scratch_shapes=[pltpu.VMEM((1280, 128), F32), pltpu.VMEM((4, 512, 128), F32)],
        name="upper_factor",
    )(mine, other)


def on_device(slab, factor):
    count, own, second, third = slab.shape
    ncol_total = count * second * lax.axis_size(WIDE) * third
    flat = slab.reshape(count, own * second, third)
    factor_t = factor.T
    acc = core = None
    chunks = []
    for c in range(count):
        parts = 2 if c == count - 1 else 1
        for k, p in enumerate(pack(flat, c, parts)):
            chunks.append((c, k * (8 // parts), p))
    for at, (c, base, p) in enumerate(chunks):
        got = [lax.ppermute(p[k], "narrow", ring(4, k)) for k in SHIFTS]
        last = at == len(chunks) - 1
        made = gram_step(c, base, [p[0]] + got, factor_t, acc, core, last)
        if last:
            mine, give, core = made
        else:
            acc, core = made
    mine, other = total(mine, give)
    r_factor = upper_factor(mine, other, 1.0 / ncol_total)
    return (r_factor, core.reshape(count, 64, second, 64))


def solution(mesh):
    narrow = mesh.shape["narrow"]
    fine = Mesh(mesh.devices.reshape(4, 4, 2, narrow), WIDE + ("narrow",))
    return jax.shard_map(
        on_device,
        mesh=fine,
        in_specs=(P(None, "narrow", WIDE, None), P()),
        out_specs=(P(), P(None, None, WIDE, "narrow")),
        check_vma=False,
    )
```

```python
import functools
import jax
import jax.numpy as jnp
from jax import lax
from jax.experimental import pallas as pl
from jax.experimental.pallas import tpu as pltpu
from jax.sharding import Mesh, PartitionSpec as P

HI = lax.Precision.HIGHEST
BLOCKS = [(i, j) for i in range(4) for j in range(i, 4)]
SHIFTS = (1, 3, 2)
FULL = [(0, 8)]
HALVES = [(0, 4), (4, 4)]
PLAN = [(0, FULL), (1, FULL), (2, FULL), (3, HALVES)]
HALF = 640
WIDE = ("z", "y", "core")
PANEL = 8
F32 = jnp.float32
BF16 = jnp.bfloat16


def ring(size, shift):
    return [(i, (i + shift) % size) for i in range(size)]


def pack_kernel(ranges, x0_ref, x1_ref, *outs):
    n = lax.axis_index("narrow")
    rows = x0_ref.shape[0] // 16
    low = lax.broadcasted_iota(jnp.int32, (rows, 128), 1) < 64

    def body(k):
        for part, (base, depth) in enumerate(ranges):

            @pl.loop(0, depth)
            def _(a):
                at = base + a
                for tile, x_ref in enumerate((x0_ref, x1_ref)):
                    lo = x_ref[pl.ds(at, rows, stride=16), :]
                    hi = x_ref[pl.ds(at + 8, rows, stride=16), :]
                    even = jnp.where(low, lo, pltpu.roll(hi, 64, 1))
                    odd = jnp.where(low, pltpu.roll(lo, 64, 1), hi)
                    outs[4 * part + (2 * tile - k) % 4][a] = even
                    outs[4 * part + (2 * tile + 1 - k) % 4][a] = odd

    for k in range(4):
        pl.when(n == k)(functools.partial(body, k))


def pack(slab, comp, ranges):
    rows = 1024
    shapes = [(d, 128, 128) for _, d in ranges for _ in range(4)]
    outs = pl.pallas_call(
        functools.partial(pack_kernel, ranges),
        grid=(2,),
        in_specs=[
            pl.BlockSpec((None, rows, 128), lambda i: (comp, i, 0)),
            pl.BlockSpec((None, rows, 128), lambda i: (comp, i, 1)),
        ],
        out_specs=[
            pl.BlockSpec((d, rows // 16, 128), lambda i: (0, i, 0)) for d, _, _ in shapes
        ],
        out_shape=[jax.ShapeDtypeStruct(shape, F32) for shape in shapes],
        cost_estimate=pl.CostEstimate(
            flops=1 << 20, bytes_accessed=4 << 20, transcendentals=0
        ),
        name="pack",
    )(slab, slab)
    return [outs[4 * k:4 * k + 4] for k in range(len(ranges))]


def split(x):
    h = x.astype(BF16)
    rest = x - h.astype(F32)
    m = rest.astype(BF16)
    l = (rest - m.astype(F32)).astype(BF16)
    return h, m, l


def nt(a, b):
    return lax.dot_general(a, b, (((1,), (1,)), ((), ())), preferred_element_type=F32)


def gram_kernel(first, last, merge, base, *refs):
    own, r1, r3, r2, factor_ref = refs[:5]
    refs = refs[5:]
    acc_in = None
    if not first:
        acc_in, core_in = refs[:2]
        refs = refs[2:]
    if last:
        mine_ref, give_ref, core_ref, h_scr, m_scr, l_scr, core_scr, acc_ref = refs
    else:
        acc_ref, core_ref, h_scr, m_scr, l_scr, core_scr = refs
    me = lax.axis_index("narrow")
    step = pl.program_id(0)
    for shift, piece in ((0, own), (1, r1), (3, r3), (2, r2)):
        row = pl.multiple_of(lax.rem(me + 4 - shift, 4) * 128, 128)
        for a in range(own.shape[0]):
            h, m, l = split(piece[a])
            lanes = slice(a * 128, (a + 1) * 128)
            h_scr[pl.ds(row, 128), lanes] = h
            m_scr[pl.ds(row, 128), lanes] = m
            l_scr[pl.ds(row, 128), lanes] = l

    @pl.when(step == 0)
    def _():
        if first:
            acc_ref[...] = jnp.zeros_like(acc_ref)
        else:
            acc_ref[...] = acc_in[...]
        if merge:
            core_scr[:, :64] = core_in[...]

    for top, side in ((256, 0), (512, 256)):
        a = [s[:top, :] for s in (h_scr, m_scr, l_scr)]
        b = [s[side:side + 256, :] for s in (h_scr, m_scr, l_scr)]
        part = nt(a[1], b[1])
        part += nt(a[0], b[2])
        part += nt(a[2], b[0])
        part += nt(a[0], b[1])
        part += nt(a[1], b[0])
        part += nt(a[0], b[0])
        for k, (i, j) in enumerate(BLOCKS):
            if side <= j * 128 < side + 256:
                acc_ref[k * 128:(k + 1) * 128, :] += part[
                    i * 128:(i + 1) * 128, j * 128 - side:j * 128 - side + 128
                ]
    f = jnp.concatenate(split(factor_ref[...]), axis=0)
    by_h = jnp.dot(f, h_scr[...], preferred_element_type=F32)
    by_m = jnp.dot(f[:128], m_scr[...], preferred_element_type=F32)
    by_l = jnp.dot(f[:64], l_scr[...], preferred_element_type=F32)
    core = (by_h[128:] + by_l + by_m[64:]) + (by_h[64:128] + by_m[:64]) + by_h[:64]
    depth = own.shape[0]
    for a in range(depth):
        part = core[:, a * 128:(a + 1) * 128]
        at = base + depth * step + a
        core_scr[pl.ds(at, 64, stride=16), :] = part
        core_scr[pl.ds(at + 8, 64, stride=16), :] = pltpu.roll(part, 64, 1)

    @pl.when(step == pl.num_programs(0) - 1)
    def _():
        core_ref[...] = core_scr[:, :64]
        if last:
            c = lax.axis_index("core")
            mine_ref[...] = acc_ref[pl.ds(pl.multiple_of(c * HALF, 128), HALF), :]
            give_ref[...] = acc_ref[pl.ds(pl.multiple_of((1 - c) * HALF, 128), HALF), :]


def gram_step(comp, base, pieces, factor_t, acc, core, last):
    first = acc is None
    merge = base > 0
    depth = pieces[0].shape[0]
    take = min(depth, 4)
    piece_spec = pl.BlockSpec((take, 128, 128), lambda s: (s, 0, 0))
    whole = lambda s: (0, 0)
    in_specs = [piece_spec] * 4 + [pl.BlockSpec((64, 512), whole)]
    core_spec = pl.BlockSpec((None, 1024, 64), lambda s: (comp, 0, 0))
    args = list(pieces) + [factor_t]
    aliases = {}
    if not first:
        in_specs += [
            pl.BlockSpec((1280, 128), whole),
            core_spec if merge else pl.BlockSpec(memory_space=pl.ANY),
        ]
        args += [acc, core]
        aliases = {6: 2} if last else {5: 0, 6: 1}
    sums = [HALF, HALF] if last else [1280]
    scratch = [pltpu.VMEM((512, 128 * take), BF16)] * 3 + [pltpu.VMEM((1024, 128), F32)]
    if last:
        scratch.append(pltpu.VMEM((1280, 128), F32))
    return pl.pallas_call(
        functools.partial(gram_kernel, first, last, merge, base),
        grid=(depth // take,),
        in_specs=in_specs,
        out_specs=[pl.BlockSpec((r, 128), whole) for r in sums] + [core_spec],
        out_shape=[jax.ShapeDtypeStruct((r, 128), F32) for r in sums]
        + [jax.ShapeDtypeStruct((4, 1024, 64), F32)],
        scratch_shapes=scratch,
        input_output_aliases=aliases,
        compiler_params=pltpu.CompilerParams(vmem_limit_bytes=40 << 20),
        cost_estimate=pl.CostEstimate(
            flops=(6 << 26) * depth, bytes_accessed=depth << 19, transcendentals=0
        ),
        name="gram",
    )(*args)


def total(mine, give):
    swap = [(0, 1), (1, 0)]
    plane = lax.axis_size("z") * lax.axis_size("y")
    h = mine + lax.ppermute(give, "core", swap)
    h = h.reshape(plane, HALF // plane, 128)
    deal = lambda x, axes: lax.all_to_all(x, axes, 0, 0, tiled=True)
    spread = lambda x, n: jnp.broadcast_to(x[None], (n,) + x.shape)
    piece = jnp.sum(deal(h, ("z", "y")), axis=0)
    for flip in (1, 3):
        piece += lax.ppermute(piece, "narrow", [(i, i ^ flip) for i in range(4)])
    h = deal(spread(piece, plane), ("z", "y")).reshape(HALF, 128)
    return h, lax.ppermute(h, "core", swap)


def factor_block(work, out_ref, b, tiles):
    lane = lax.broadcasted_iota(jnp.int32, (8, 128), 1)
    sub = lax.broadcasted_iota(jnp.int32, (8, 128), 0)
    base = b * 128
    spread = lambda v, i: jnp.broadcast_to(v[i:i + 1, :], (8, 128))
    column = lambda v, j: jnp.broadcast_to(v[:, j:j + 1], (8, 128))
    for p in range(16):
        at = base + 8 * p
        head = work[b, at:at + 8, :]
        if p % PANEL == 0:
            cols = [column(head, 8 * p + j) for j in range(8)]
        else:
            cols = ncols
        last = p - p % PANEL + PANEL
        more = p + 1 < last
        if more:
            nxt = work[b, at + 8:at + 16, :]
            ncols = [column(nxt, 8 * (p + 1) + j) for j in range(8)]
        c = {(i, j): spread(cols[j], i) for j in range(8) for i in range(j + 1)}
        rs, u = [], {}
        for k in range(8):
            r = lax.rsqrt(c[k, k])
            rs.append(r)
            for j in range(k + 1, 8):
                u[k, j] = c[k, j] * r
            for j in range(k + 1, 8):
                for i in range(k + 1, j + 1):
                    c[i, j] = c[i, j] - u[k, i] * u[k, j]
        rows = {}
        for t in tiles:
            x = head if t == b else work[t, at:at + 8, :]
            made = []
            for k in range(8):
                v = spread(x, k)
                for m in range(k):
                    v = v - u[m, k] * made[m]
                made.append(v * rs[k])
            rows[t] = made
            full = made[0]
            for k in range(1, 8):
                full = jnp.where(sub >= k, made[k], full)
            if t == b:
                full = jnp.where(lane >= sub + 8 * p, full, 0.0)
            out_ref[at:at + 8, t * 128:(t + 1) * 128] = full
        for g in range(p + 1, last):
            ag = base + 8 * g
            a = work[b, ag:ag + 8, :]
            left = [column(a, 8 * p + j) for j in range(8)]
            ug = []
            for k in range(8):
                w = left[k] * rs[k]
                ug.append(w)
                for j in range(k + 1, 8):
                    left[j] = left[j] - w * u[k, j]
                if more and g == p + 1:
                    for j in range(8):
                        ncols[j] = ncols[j] - w * spread(w, j)
            for t in tiles:
                v = a if t == b else work[t, ag:ag + 8, :]
                for k in range(8):
                    v = v - ug[k] * rows[t][k]
                work[t, ag:ag + 8, :] = v
        if p + 1 == last and last < 16:
            done = out_ref[at + 8 - 8 * PANEL:at + 8, base:]
            part = lax.dot_general(
                done[:, :128], done, (((0,), (0,)), ((), ())),
                precision=HI, preferred_element_type=F32,
            )
            for t in tiles:
                o = (t - b) * 128
                work[t, base + 8 * last:base + 128, :] -= part[8 * last:, o:o + 128]


def chol_kernel(scale, mine_ref, other_ref, out_ref, gram, work):
    c = lax.axis_index("core")
    gram[pl.ds(pl.multiple_of(c * HALF, 128), HALF), :] = mine_ref[...]
    gram[pl.ds(pl.multiple_of((1 - c) * HALF, 128), HALF), :] = other_ref[...]
    for k, (i, j) in enumerate(BLOCKS):
        work[j, i * 128:(i + 1) * 128, :] = gram[k * 128:(k + 1) * 128, :] * scale
    for b in range(4):
        factor_block(work, out_ref, b, range(b, 4))
        for t in range(b):
            out_ref[b * 128:(b + 1) * 128, t * 128:(t + 1) * 128] = jnp.zeros((128, 128), F32)
        if b < 3:
            tail = out_ref[b * 128:(b + 1) * 128, (b + 1) * 128:]
            for i in range(b + 1, 4):
                o = (i - b - 1) * 128
                part = lax.dot_general(
                    tail[:, o:o + 128],
                    tail[:, o:],
                    (((0,), (0,)), ((), ())),
                    precision=HI,
                    preferred_element_type=F32,
                )
                for j in range(i, 4):
                    work[j, i * 128:(i + 1) * 128, :] -= part[:, (j - i) * 128:(j - i + 1) * 128]


def upper_factor(mine, other, scale):
    return pl.pallas_call(
        functools.partial(chol_kernel, scale),
        out_shape=jax.ShapeDtypeStruct((512, 512), F32),
        in_specs=[pl.BlockSpec((HALF, 128), lambda: (0, 0))] * 2,
        out_specs=pl.BlockSpec((512, 512), lambda: (0, 0)),
        scratch_shapes=[pltpu.VMEM((1280, 128), F32), pltpu.VMEM((4, 512, 128), F32)],
        name="upper_factor",
    )(mine, other)


def on_device(slab, factor):
    count, own, second, third = slab.shape
    ncol_total = count * second * lax.axis_size(WIDE) * third
    flat = slab.reshape(count, own * second, third)
    factor_t = factor.T
    acc = core = None
    chunks = []
    for comp, ranges in PLAN:
        for (base, _), p in zip(ranges, pack(flat, comp, ranges)):
            chunks.append((comp, base, p))
    arrived = []
    for at, (c, base, p) in enumerate(chunks):
        arrived.append([lax.ppermute(p[k], "narrow", ring(4, k)) for k in SHIFTS])
    for at, (c, base, p) in enumerate(chunks):
        last = at == len(chunks) - 1
        made = gram_step(c, base, [p[0]] + arrived[at], factor_t, acc, core, last)
        if last:
            mine, give, core = made
        else:
            acc, core = made
    mine, other = total(mine, give)
    r_factor = upper_factor(mine, other, 1.0 / ncol_total)
    return (r_factor, core.reshape(count, 64, second, 64))


def solution(mesh):
    narrow = mesh.shape["narrow"]
    fine = Mesh(mesh.devices.reshape(4, 4, 2, narrow), WIDE + ("narrow",))
    return jax.shard_map(
        on_device,
        mesh=fine,
        in_specs=(P(None, "narrow", WIDE, None), P()),
        out_specs=(P(), P(None, None, WIDE, "narrow")),
        check_vma=False,
    )
```

```python
import functools
import jax
import jax.numpy as jnp
from jax import lax
from jax.experimental import pallas as pl
from jax.experimental.pallas import tpu as pltpu
from jax.sharding import Mesh, PartitionSpec as P

HI = lax.Precision.HIGHEST
BLOCKS = [(i, j) for i in range(4) for j in range(i, 4)]
SHIFTS = (1, 3, 2)
FULL = [(0, 8)]
HALVES = [(0, 4), (4, 4)]
PLAN = [(0, FULL), (1, FULL), (2, FULL), (3, [(0, 6), (6, 2)])]
HALF = 640
WIDE = ("z", "y", "core")
PANEL = 8
F32 = jnp.float32
BF16 = jnp.bfloat16


def ring(size, shift):
    return [(i, (i + shift) % size) for i in range(size)]


def pack_kernel(ranges, x0_ref, x1_ref, *outs):
    n = lax.axis_index("narrow")
    rows = x0_ref.shape[0] // 16
    low = lax.broadcasted_iota(jnp.int32, (rows, 128), 1) < 64

    def body(k):
        for part, (base, depth) in enumerate(ranges):

            @pl.loop(0, depth)
            def _(a):
                at = base + a
                for tile, x_ref in enumerate((x0_ref, x1_ref)):
                    lo = x_ref[pl.ds(at, rows, stride=16), :]
                    hi = x_ref[pl.ds(at + 8, rows, stride=16), :]
                    even = jnp.where(low, lo, pltpu.roll(hi, 64, 1))
                    odd = jnp.where(low, pltpu.roll(lo, 64, 1), hi)
                    outs[4 * part + (2 * tile - k) % 4][a] = even
                    outs[4 * part + (2 * tile + 1 - k) % 4][a] = odd

    for k in range(4):
        pl.when(n == k)(functools.partial(body, k))


def pack(slab, comp, ranges):
    rows = 1024
    shapes = [(d, 128, 128) for _, d in ranges for _ in range(4)]
    outs = pl.pallas_call(
        functools.partial(pack_kernel, ranges),
        grid=(2,),
        in_specs=[
            pl.BlockSpec((None, rows, 128), lambda i: (comp, i, 0)),
            pl.BlockSpec((None, rows, 128), lambda i: (comp, i, 1)),
        ],
        out_specs=[
            pl.BlockSpec((d, rows // 16, 128), lambda i: (0, i, 0)) for d, _, _ in shapes
        ],
        out_shape=[jax.ShapeDtypeStruct(shape, F32) for shape in shapes],
        cost_estimate=pl.CostEstimate(
            flops=1 << 20, bytes_accessed=4 << 20, transcendentals=0
        ),
        name="pack",
    )(slab, slab)
    return [outs[4 * k:4 * k + 4] for k in range(len(ranges))]


def split(x):
    h = x.astype(BF16)
    rest = x - h.astype(F32)
    m = rest.astype(BF16)
    l = (rest - m.astype(F32)).astype(BF16)
    return h, m, l


def nt(a, b):
    return lax.dot_general(a, b, (((1,), (1,)), ((), ())), preferred_element_type=F32)


def gram_kernel(first, last, merge, base, *refs):
    own, r1, r3, r2, factor_ref = refs[:5]
    refs = refs[5:]
    acc_in = None
    if not first:
        acc_in, core_in = refs[:2]
        refs = refs[2:]
    if last:
        mine_ref, give_ref, core_ref, h_scr, m_scr, l_scr, core_scr, acc_ref = refs
    else:
        acc_ref, core_ref, h_scr, m_scr, l_scr, core_scr = refs
    me = lax.axis_index("narrow")
    step = pl.program_id(0)
    for shift, piece in ((0, own), (1, r1), (3, r3), (2, r2)):
        row = pl.multiple_of(lax.rem(me + 4 - shift, 4) * 128, 128)
        for a in range(own.shape[0]):
            h, m, l = split(piece[a])
            lanes = slice(a * 128, (a + 1) * 128)
            h_scr[pl.ds(row, 128), lanes] = h
            m_scr[pl.ds(row, 128), lanes] = m
            l_scr[pl.ds(row, 128), lanes] = l

    @pl.when(step == 0)
    def _():
        if first:
            acc_ref[...] = jnp.zeros_like(acc_ref)
        else:
            acc_ref[...] = acc_in[...]
        if merge:
            core_scr[:, :64] = core_in[...]

    for top, side in ((256, 0), (512, 256)):
        a = [s[:top, :] for s in (h_scr, m_scr, l_scr)]
        b = [s[side:side + 256, :] for s in (h_scr, m_scr, l_scr)]
        part = nt(a[1], b[1])
        part += nt(a[0], b[2])
        part += nt(a[2], b[0])
        part += nt(a[0], b[1])
        part += nt(a[1], b[0])
        part += nt(a[0], b[0])
        for k, (i, j) in enumerate(BLOCKS):
            if side <= j * 128 < side + 256:
                acc_ref[k * 128:(k + 1) * 128, :] += part[
                    i * 128:(i + 1) * 128, j * 128 - side:j * 128 - side + 128
                ]
    f = jnp.concatenate(split(factor_ref[...]), axis=0)
    by_h = jnp.dot(f, h_scr[...], preferred_element_type=F32)
    by_m = jnp.dot(f[:128], m_scr[...], preferred_element_type=F32)
    by_l = jnp.dot(f[:64], l_scr[...], preferred_element_type=F32)
    core = (by_h[128:] + by_l + by_m[64:]) + (by_h[64:128] + by_m[:64]) + by_h[:64]
    depth = own.shape[0]
    for a in range(depth):
        part = core[:, a * 128:(a + 1) * 128]
        at = base + depth * step + a
        core_scr[pl.ds(at, 64, stride=16), :] = part
        core_scr[pl.ds(at + 8, 64, stride=16), :] = pltpu.roll(part, 64, 1)

    @pl.when(step == pl.num_programs(0) - 1)
    def _():
        core_ref[...] = core_scr[:, :64]
        if last:
            c = lax.axis_index("core")
            mine_ref[...] = acc_ref[pl.ds(pl.multiple_of(c * HALF, 128), HALF), :]
            give_ref[...] = acc_ref[pl.ds(pl.multiple_of((1 - c) * HALF, 128), HALF), :]


def gram_step(comp, base, pieces, factor_t, acc, core, last):
    first = acc is None
    merge = base > 0
    depth = pieces[0].shape[0]
    take = 2 if depth < 4 else depth // 2
    piece_spec = pl.BlockSpec((take, 128, 128), lambda s: (s, 0, 0))
    whole = lambda s: (0, 0)
    in_specs = [piece_spec] * 4 + [pl.BlockSpec((64, 512), whole)]
    core_spec = pl.BlockSpec((None, 1024, 64), lambda s: (comp, 0, 0))
    args = list(pieces) + [factor_t]
    aliases = {}
    if not first:
        in_specs += [
            pl.BlockSpec((1280, 128), whole),
            core_spec if merge else pl.BlockSpec(memory_space=pl.ANY),
        ]
        args += [acc, core]
        aliases = {6: 2} if last else {5: 0, 6: 1}
    sums = [HALF, HALF] if last else [1280]
    scratch = [pltpu.VMEM((512, 128 * take), BF16)] * 3 + [pltpu.VMEM((1024, 128), F32)]
    if last:
        scratch.append(pltpu.VMEM((1280, 128), F32))
    return pl.pallas_call(
        functools.partial(gram_kernel, first, last, merge, base),
        grid=(depth // take,),
        in_specs=in_specs,
        out_specs=[pl.BlockSpec((r, 128), whole) for r in sums] + [core_spec],
        out_shape=[jax.ShapeDtypeStruct((r, 128), F32) for r in sums]
        + [jax.ShapeDtypeStruct((4, 1024, 64), F32)],
        scratch_shapes=scratch,
        input_output_aliases=aliases,
        compiler_params=pltpu.CompilerParams(vmem_limit_bytes=40 << 20),
        cost_estimate=pl.CostEstimate(
            flops=(6 << 26) * depth, bytes_accessed=depth << 19, transcendentals=0
        ),
        name="gram",
    )(*args)


def total(mine, give):
    swap = [(0, 1), (1, 0)]
    plane = lax.axis_size("z") * lax.axis_size("y")
    h = mine + lax.ppermute(give, "core", swap)
    h = h.reshape(plane, HALF // plane, 128)
    deal = lambda x, axes: lax.all_to_all(x, axes, 0, 0, tiled=True)
    spread = lambda x, n: jnp.broadcast_to(x[None], (n,) + x.shape)
    piece = jnp.sum(deal(h, ("z", "y")), axis=0)
    for flip in (1, 3):
        piece += lax.ppermute(piece, "narrow", [(i, i ^ flip) for i in range(4)])
    h = deal(spread(piece, plane), ("z", "y")).reshape(HALF, 128)
    return h, lax.ppermute(h, "core", swap)


def factor_block(work, out_ref, b, tiles):
    lane = lax.broadcasted_iota(jnp.int32, (8, 128), 1)
    sub = lax.broadcasted_iota(jnp.int32, (8, 128), 0)
    base = b * 128
    spread = lambda v, i: jnp.broadcast_to(v[i:i + 1, :], (8, 128))
    column = lambda v, j: jnp.broadcast_to(v[:, j:j + 1], (8, 128))
    for p in range(16):
        at = base + 8 * p
        head = work[b, at:at + 8, :]
        if p % PANEL == 0:
            cols = [column(head, 8 * p + j) for j in range(8)]
        else:
            cols = ncols
        last = p - p % PANEL + PANEL
        more = p + 1 < last
        if more:
            nxt = work[b, at + 8:at + 16, :]
            ncols = [column(nxt, 8 * (p + 1) + j) for j in range(8)]
        c = {(i, j): spread(cols[j], i) for j in range(8) for i in range(j + 1)}
        rs, u = [], {}
        for k in range(8):
            r = lax.rsqrt(c[k, k])
            rs.append(r)
            for j in range(k + 1, 8):
                u[k, j] = c[k, j] * r
            for j in range(k + 1, 8):
                for i in range(k + 1, j + 1):
                    c[i, j] = c[i, j] - u[k, i] * u[k, j]
        rows = {}
        for t in tiles:
            x = head if t == b else work[t, at:at + 8, :]
            made = []
            for k in range(8):
                v = spread(x, k)
                for m in range(k):
                    v = v - u[m, k] * made[m]
                made.append(v * rs[k])
            rows[t] = made
            full = made[0]
            for k in range(1, 8):
                full = jnp.where(sub >= k, made[k], full)
            if t == b:
                full = jnp.where(lane >= sub + 8 * p, full, 0.0)
            out_ref[at:at + 8, t * 128:(t + 1) * 128] = full
        for g in range(p + 1, last):
            ag = base + 8 * g
            a = work[b, ag:ag + 8, :]
            left = [column(a, 8 * p + j) for j in range(8)]
            ug = []
            for k in range(8):
                w = left[k] * rs[k]
                ug.append(w)
                for j in range(k + 1, 8):
                    left[j] = left[j] - w * u[k, j]
                if more and g == p + 1:
                    for j in range(8):
                        ncols[j] = ncols[j] - w * spread(w, j)
            for t in tiles:
                v = a if t == b else work[t, ag:ag + 8, :]
                for k in range(8):
                    v = v - ug[k] * rows[t][k]
                work[t, ag:ag + 8, :] = v
        if p + 1 == last and last < 16:
            done = out_ref[at + 8 - 8 * PANEL:at + 8, base:]
            part = lax.dot_general(
                done[:, :128], done, (((0,), (0,)), ((), ())),
                precision=HI, preferred_element_type=F32,
            )
            for t in tiles:
                o = (t - b) * 128
                work[t, base + 8 * last:base + 128, :] -= part[8 * last:, o:o + 128]


def chol_kernel(scale, mine_ref, other_ref, out_ref, gram, work):
    c = lax.axis_index("core")
    gram[pl.ds(pl.multiple_of(c * HALF, 128), HALF), :] = mine_ref[...]
    gram[pl.ds(pl.multiple_of((1 - c) * HALF, 128), HALF), :] = other_ref[...]
    for k, (i, j) in enumerate(BLOCKS):
        work[j, i * 128:(i + 1) * 128, :] = gram[k * 128:(k + 1) * 128, :] * scale
    for b in range(4):
        factor_block(work, out_ref, b, range(b, 4))
        for t in range(b):
            out_ref[b * 128:(b + 1) * 128, t * 128:(t + 1) * 128] = jnp.zeros((128, 128), F32)
        if b < 3:
            tail = out_ref[b * 128:(b + 1) * 128, (b + 1) * 128:]
            for i in range(b + 1, 4):
                o = (i - b - 1) * 128
                part = lax.dot_general(
                    tail[:, o:o + 128],
                    tail[:, o:],
                    (((0,), (0,)), ((), ())),
                    precision=HI,
                    preferred_element_type=F32,
                )
                for j in range(i, 4):
                    work[j, i * 128:(i + 1) * 128, :] -= part[:, (j - i) * 128:(j - i + 1) * 128]


def upper_factor(mine, other, scale):
    return pl.pallas_call(
        functools.partial(chol_kernel, scale),
        out_shape=jax.ShapeDtypeStruct((512, 512), F32),
        in_specs=[pl.BlockSpec((HALF, 128), lambda: (0, 0))] * 2,
        out_specs=pl.BlockSpec((512, 512), lambda: (0, 0)),
        scratch_shapes=[pltpu.VMEM((1280, 128), F32), pltpu.VMEM((4, 512, 128), F32)],
        name="upper_factor",
    )(mine, other)


def on_device(slab, factor):
    count, own, second, third = slab.shape
    ncol_total = count * second * lax.axis_size(WIDE) * third
    flat = slab.reshape(count, own * second, third)
    factor_t = factor.T
    acc = core = None
    chunks = []
    for comp, ranges in PLAN:
        for (base, _), p in zip(ranges, pack(flat, comp, ranges)):
            chunks.append((comp, base, p))
    arrived = []
    for at, (c, base, p) in enumerate(chunks):
        arrived.append([lax.ppermute(p[k], "narrow", ring(4, k)) for k in SHIFTS])
    for at, (c, base, p) in enumerate(chunks):
        last = at == len(chunks) - 1
        made = gram_step(c, base, [p[0]] + arrived[at], factor_t, acc, core, last)
        if last:
            mine, give, core = made
        else:
            acc, core = made
    mine, other = total(mine, give)
    r_factor = upper_factor(mine, other, 1.0 / ncol_total)
    return (r_factor, core.reshape(count, 64, second, 64))


def solution(mesh):
    narrow = mesh.shape["narrow"]
    fine = Mesh(mesh.devices.reshape(4, 4, 2, narrow), WIDE + ("narrow",))
    return jax.shard_map(
        on_device,
        mesh=fine,
        in_specs=(P(None, "narrow", WIDE, None), P()),
        out_specs=(P(), P(None, None, WIDE, "narrow")),
        check_vma=False,
    )
```

```python
import functools
import jax
import jax.numpy as jnp
from jax import lax
from jax.experimental import pallas as pl
from jax.experimental.pallas import tpu as pltpu
from jax.sharding import Mesh, PartitionSpec as P

HI = lax.Precision.HIGHEST
BLOCKS = [(i, j) for i in range(4) for j in range(i, 4)]
SHIFTS = (1, 3, 2)
FULL = [(0, 8)]
HALVES = [(0, 4), (4, 4)]
PLAN = [(0, FULL), (1, FULL), (2, FULL), (3, [(0, 6), (6, 2)])]
HALF = 640
WIDE = ("z", "y", "core")
PANEL = 8
F32 = jnp.float32
BF16 = jnp.bfloat16


def ring(size, shift):
    return [(i, (i + shift) % size) for i in range(size)]


def pack_kernel(ranges, x0_ref, x1_ref, *outs):
    n = lax.axis_index("narrow")
    rows = x0_ref.shape[0] // 16
    low = lax.broadcasted_iota(jnp.int32, (rows, 128), 1) < 64

    def body(k):
        for part, (base, depth) in enumerate(ranges):

            @pl.loop(0, depth)
            def _(a):
                at = base + a
                for tile, x_ref in enumerate((x0_ref, x1_ref)):
                    lo = x_ref[pl.ds(at, rows, stride=16), :]
                    hi = x_ref[pl.ds(at + 8, rows, stride=16), :]
                    even = jnp.where(low, lo, pltpu.roll(hi, 64, 1))
                    odd = jnp.where(low, pltpu.roll(lo, 64, 1), hi)
                    outs[4 * part + (2 * tile - k) % 4][a] = even
                    outs[4 * part + (2 * tile + 1 - k) % 4][a] = odd

    for k in range(4):
        pl.when(n == k)(functools.partial(body, k))


def pack(slab, comp, ranges):
    rows = 2048
    shapes = [(d, 128, 128) for _, d in ranges for _ in range(4)]
    outs = pl.pallas_call(
        functools.partial(pack_kernel, ranges),
        grid=(1,),
        in_specs=[
            pl.BlockSpec((None, rows, 128), lambda i: (comp, i, 0)),
            pl.BlockSpec((None, rows, 128), lambda i: (comp, i, 1)),
        ],
        out_specs=[
            pl.BlockSpec((d, rows // 16, 128), lambda i: (0, i, 0)) for d, _, _ in shapes
        ],
        out_shape=[jax.ShapeDtypeStruct(shape, F32) for shape in shapes],
        cost_estimate=pl.CostEstimate(
            flops=1 << 20, bytes_accessed=4 << 20, transcendentals=0
        ),
        name="pack",
    )(slab, slab)
    return [outs[4 * k:4 * k + 4] for k in range(len(ranges))]


def split(x):
    h = x.astype(BF16)
    rest = x - h.astype(F32)
    m = rest.astype(BF16)
    l = (rest - m.astype(F32)).astype(BF16)
    return h, m, l


def nt(a, b):
    return lax.dot_general(a, b, (((1,), (1,)), ((), ())), preferred_element_type=F32)


def gram_kernel(first, last, merge, base, *refs):
    own, r1, r3, r2, factor_ref = refs[:5]
    refs = refs[5:]
    acc_in = None
    if not first:
        acc_in, core_in = refs[:2]
        refs = refs[2:]
    if last:
        mine_ref, give_ref, core_ref, h_scr, m_scr, l_scr, core_scr, acc_ref = refs
    else:
        acc_ref, core_ref, h_scr, m_scr, l_scr, core_scr = refs
    me = lax.axis_index("narrow")
    step = pl.program_id(0)
    for shift, piece in ((0, own), (1, r1), (3, r3), (2, r2)):
        row = pl.multiple_of(lax.rem(me + 4 - shift, 4) * 128, 128)
        for a in range(own.shape[0]):
            h, m, l = split(piece[a])
            lanes = slice(a * 128, (a + 1) * 128)
            h_scr[pl.ds(row, 128), lanes] = h
            m_scr[pl.ds(row, 128), lanes] = m
            l_scr[pl.ds(row, 128), lanes] = l

    @pl.when(step == 0)
    def _():
        if first:
            acc_ref[...] = jnp.zeros_like(acc_ref)
        else:
            acc_ref[...] = acc_in[...]
        if merge:
            core_scr[:, :64] = core_in[...]

    for top, side in ((256, 0), (512, 256)):
        a = [s[:top, :] for s in (h_scr, m_scr, l_scr)]
        b = [s[side:side + 256, :] for s in (h_scr, m_scr, l_scr)]
        part = nt(a[1], b[1])
        part += nt(a[0], b[2])
        part += nt(a[2], b[0])
        part += nt(a[0], b[1])
        part += nt(a[1], b[0])
        part += nt(a[0], b[0])
        for k, (i, j) in enumerate(BLOCKS):
            if side <= j * 128 < side + 256:
                acc_ref[k * 128:(k + 1) * 128, :] += part[
                    i * 128:(i + 1) * 128, j * 128 - side:j * 128 - side + 128
                ]
    f = jnp.concatenate(split(factor_ref[...]), axis=0)
    by_h = jnp.dot(f, h_scr[...], preferred_element_type=F32)
    by_m = jnp.dot(f[:128], m_scr[...], preferred_element_type=F32)
    by_l = jnp.dot(f[:64], l_scr[...], preferred_element_type=F32)
    core = (by_h[128:] + by_l + by_m[64:]) + (by_h[64:128] + by_m[:64]) + by_h[:64]
    depth = own.shape[0]
    for a in range(depth):
        part = core[:, a * 128:(a + 1) * 128]
        at = base + depth * step + a
        core_scr[pl.ds(at, 64, stride=16), :] = part
        core_scr[pl.ds(at + 8, 64, stride=16), :] = pltpu.roll(part, 64, 1)

    @pl.when(step == pl.num_programs(0) - 1)
    def _():
        core_ref[...] = core_scr[:, :64]
        if last:
            c = lax.axis_index("core")
            mine_ref[...] = acc_ref[pl.ds(pl.multiple_of(c * HALF, 128), HALF), :]
            give_ref[...] = acc_ref[pl.ds(pl.multiple_of((1 - c) * HALF, 128), HALF), :]


def gram_step(comp, base, pieces, factor_t, acc, core, last):
    first = acc is None
    merge = base > 0
    depth = pieces[0].shape[0]
    take = 2 if depth < 4 else depth // 2
    piece_spec = pl.BlockSpec((take, 128, 128), lambda s: (s, 0, 0))
    whole = lambda s: (0, 0)
    in_specs = [piece_spec] * 4 + [pl.BlockSpec((64, 512), whole)]
    core_spec = pl.BlockSpec((None, 1024, 64), lambda s: (comp, 0, 0))
    args = list(pieces) + [factor_t]
    aliases = {}
    if not first:
        in_specs += [
            pl.BlockSpec((1280, 128), whole),
            core_spec if merge else pl.BlockSpec(memory_space=pl.ANY),
        ]
        args += [acc, core]
        aliases = {6: 2} if last else {5: 0, 6: 1}
    sums = [HALF, HALF] if last else [1280]
    scratch = [pltpu.VMEM((512, 128 * take), BF16)] * 3 + [pltpu.VMEM((1024, 128), F32)]
    if last:
        scratch.append(pltpu.VMEM((1280, 128), F32))
    return pl.pallas_call(
        functools.partial(gram_kernel, first, last, merge, base),
        grid=(depth // take,),
        in_specs=in_specs,
        out_specs=[pl.BlockSpec((r, 128), whole) for r in sums] + [core_spec],
        out_shape=[jax.ShapeDtypeStruct((r, 128), F32) for r in sums]
        + [jax.ShapeDtypeStruct((4, 1024, 64), F32)],
        scratch_shapes=scratch,
        input_output_aliases=aliases,
        compiler_params=pltpu.CompilerParams(vmem_limit_bytes=40 << 20),
        cost_estimate=pl.CostEstimate(
            flops=(6 << 26) * depth, bytes_accessed=depth << 19, transcendentals=0
        ),
        name="gram",
    )(*args)


def total(mine, give):
    swap = [(0, 1), (1, 0)]
    plane = lax.axis_size("z") * lax.axis_size("y")
    h = mine + lax.ppermute(give, "core", swap)
    h = h.reshape(plane, HALF // plane, 128)
    deal = lambda x, axes: lax.all_to_all(x, axes, 0, 0, tiled=True)
    spread = lambda x, n: jnp.broadcast_to(x[None], (n,) + x.shape)
    piece = jnp.sum(deal(h, ("z", "y")), axis=0)
    for flip in (1, 3):
        piece += lax.ppermute(piece, "narrow", [(i, i ^ flip) for i in range(4)])
    h = deal(spread(piece, plane), ("z", "y")).reshape(HALF, 128)
    return h, lax.ppermute(h, "core", swap)


def factor_block(work, out_ref, b, tiles):
    lane = lax.broadcasted_iota(jnp.int32, (8, 128), 1)
    sub = lax.broadcasted_iota(jnp.int32, (8, 128), 0)
    base = b * 128
    spread = lambda v, i: jnp.broadcast_to(v[i:i + 1, :], (8, 128))
    column = lambda v, j: jnp.broadcast_to(v[:, j:j + 1], (8, 128))
    for p in range(16):
        at = base + 8 * p
        head = work[b, at:at + 8, :]
        if p % PANEL == 0:
            cols = [column(head, 8 * p + j) for j in range(8)]
        else:
            cols = ncols
        last = p - p % PANEL + PANEL
        more = p + 1 < last
        if more:
            nxt = work[b, at + 8:at + 16, :]
            ncols = [column(nxt, 8 * (p + 1) + j) for j in range(8)]
        c = {(i, j): spread(cols[j], i) for j in range(8) for i in range(j + 1)}
        rs, u = [], {}
        for k in range(8):
            r = lax.rsqrt(c[k, k])
            rs.append(r)
            for j in range(k + 1, 8):
                u[k, j] = c[k, j] * r
            for j in range(k + 1, 8):
                for i in range(k + 1, j + 1):
                    c[i, j] = c[i, j] - u[k, i] * u[k, j]
        rows = {}
        for t in tiles:
            x = head if t == b else work[t, at:at + 8, :]
            made = []
            for k in range(8):
                v = spread(x, k)
                for m in range(k):
                    v = v - u[m, k] * made[m]
                made.append(v * rs[k])
            rows[t] = made
            full = made[0]
            for k in range(1, 8):
                full = jnp.where(sub >= k, made[k], full)
            if t == b:
                full = jnp.where(lane >= sub + 8 * p, full, 0.0)
            out_ref[at:at + 8, t * 128:(t + 1) * 128] = full
        for g in range(p + 1, last):
            ag = base + 8 * g
            a = work[b, ag:ag + 8, :]
            left = [column(a, 8 * p + j) for j in range(8)]
            ug = []
            for k in range(8):
                w = left[k] * rs[k]
                ug.append(w)
                for j in range(k + 1, 8):
                    left[j] = left[j] - w * u[k, j]
                if more and g == p + 1:
                    for j in range(8):
                        ncols[j] = ncols[j] - w * spread(w, j)
            for t in tiles:
                v = a if t == b else work[t, ag:ag + 8, :]
                for k in range(8):
                    v = v - ug[k] * rows[t][k]
                work[t, ag:ag + 8, :] = v
        if p + 1 == last and last < 16:
            done = out_ref[at + 8 - 8 * PANEL:at + 8, base:]
            part = lax.dot_general(
                done[:, :128], done, (((0,), (0,)), ((), ())),
                precision=HI, preferred_element_type=F32,
            )
            for t in tiles:
                o = (t - b) * 128
                work[t, base + 8 * last:base + 128, :] -= part[8 * last:, o:o + 128]


def chol_kernel(scale, mine_ref, other_ref, out_ref, gram, work):
    c = lax.axis_index("core")
    gram[pl.ds(pl.multiple_of(c * HALF, 128), HALF), :] = mine_ref[...]
    gram[pl.ds(pl.multiple_of((1 - c) * HALF, 128), HALF), :] = other_ref[...]
    for k, (i, j) in enumerate(BLOCKS):
        work[j, i * 128:(i + 1) * 128, :] = gram[k * 128:(k + 1) * 128, :] * scale
    for b in range(4):
        factor_block(work, out_ref, b, range(b, 4))
        for t in range(b):
            out_ref[b * 128:(b + 1) * 128, t * 128:(t + 1) * 128] = jnp.zeros((128, 128), F32)
        if b < 3:
            tail = out_ref[b * 128:(b + 1) * 128, (b + 1) * 128:]
            for i in range(b + 1, 4):
                o = (i - b - 1) * 128
                part = lax.dot_general(
                    tail[:, o:o + 128],
                    tail[:, o:],
                    (((0,), (0,)), ((), ())),
                    precision=HI,
                    preferred_element_type=F32,
                )
                for j in range(i, 4):
                    work[j, i * 128:(i + 1) * 128, :] -= part[:, (j - i) * 128:(j - i + 1) * 128]


def upper_factor(mine, other, scale):
    return pl.pallas_call(
        functools.partial(chol_kernel, scale),
        out_shape=jax.ShapeDtypeStruct((512, 512), F32),
        in_specs=[pl.BlockSpec((HALF, 128), lambda: (0, 0))] * 2,
        out_specs=pl.BlockSpec((512, 512), lambda: (0, 0)),
        scratch_shapes=[pltpu.VMEM((1280, 128), F32), pltpu.VMEM((4, 512, 128), F32)],
        name="upper_factor",
    )(mine, other)


def on_device(slab, factor):
    count, own, second, third = slab.shape
    ncol_total = count * second * lax.axis_size(WIDE) * third
    flat = slab.reshape(count, own * second, third)
    factor_t = factor.T
    acc = core = None
    chunks = []
    for comp, ranges in PLAN:
        for (base, _), p in zip(ranges, pack(flat, comp, ranges)):
            chunks.append((comp, base, p))
    arrived = []
    for at, (c, base, p) in enumerate(chunks):
        arrived.append([lax.ppermute(p[k], "narrow", ring(4, k)) for k in SHIFTS])
    for at, (c, base, p) in enumerate(chunks):
        last = at == len(chunks) - 1
        made = gram_step(c, base, [p[0]] + arrived[at], factor_t, acc, core, last)
        if last:
            mine, give, core = made
        else:
            acc, core = made
    mine, other = total(mine, give)
    r_factor = upper_factor(mine, other, 1.0 / ncol_total)
    return (r_factor, core.reshape(count, 64, second, 64))


def solution(mesh):
    narrow = mesh.shape["narrow"]
    fine = Mesh(mesh.devices.reshape(4, 4, 2, narrow), WIDE + ("narrow",))
    return jax.shard_map(
        on_device,
        mesh=fine,
        in_specs=(P(None, "narrow", WIDE, None), P()),
        out_specs=(P(), P(None, None, WIDE, "narrow")),
        check_vma=False,
    )
```

```python
import functools
import jax
import jax.numpy as jnp
from jax import lax
from jax.experimental import pallas as pl
from jax.experimental.pallas import tpu as pltpu
from jax.sharding import Mesh, PartitionSpec as P

HI = lax.Precision.HIGHEST
BLOCKS = [(i, j) for i in range(4) for j in range(i, 4)]
SHIFTS = (1, 3, 2)
FULL = [(0, 8)]
HALVES = [(0, 4), (4, 4)]
PLAN = [(0, FULL), (1, FULL), (2, FULL), (3, [(0, 6), (6, 2)])]
HALF = 640
WIDE = ("z", "y", "core")
PANEL = 8
F32 = jnp.float32
BF16 = jnp.bfloat16


def ring(size, shift):
    return [(i, (i + shift) % size) for i in range(size)]


def pack_kernel(ranges, x0_ref, x1_ref, *outs):
    n = lax.axis_index("narrow")
    rows = x0_ref.shape[0] // 16
    low = lax.broadcasted_iota(jnp.int32, (rows, 128), 1) < 64

    def body(k):
        for part, (base, depth) in enumerate(ranges):

            @pl.loop(0, depth)
            def _(a):
                at = base + a
                for tile, x_ref in enumerate((x0_ref, x1_ref)):
                    lo = x_ref[pl.ds(at, rows, stride=16), :]
                    hi = x_ref[pl.ds(at + 8, rows, stride=16), :]
                    even = jnp.where(low, lo, pltpu.roll(hi, 64, 1))
                    odd = jnp.where(low, pltpu.roll(lo, 64, 1), hi)
                    outs[4 * part + (2 * tile - k) % 4][a] = even
                    outs[4 * part + (2 * tile + 1 - k) % 4][a] = odd

    for k in range(4):
        pl.when(n == k)(functools.partial(body, k))


def pack(slab, comp, ranges):
    rows = 2048
    shapes = [(d, 128, 128) for _, d in ranges for _ in range(4)]
    outs = pl.pallas_call(
        functools.partial(pack_kernel, ranges),
        grid=(1,),
        in_specs=[
            pl.BlockSpec((None, rows, 128), lambda i: (comp, i, 0)),
            pl.BlockSpec((None, rows, 128), lambda i: (comp, i, 1)),
        ],
        out_specs=[
            pl.BlockSpec((d, rows // 16, 128), lambda i: (0, i, 0)) for d, _, _ in shapes
        ],
        out_shape=[jax.ShapeDtypeStruct(shape, F32) for shape in shapes],
        cost_estimate=pl.CostEstimate(
            flops=1 << 20, bytes_accessed=4 << 20, transcendentals=0
        ),
        name="pack",
    )(slab, slab)
    return [outs[4 * k:4 * k + 4] for k in range(len(ranges))]


def split(x):
    h = x.astype(BF16)
    rest = x - h.astype(F32)
    m = rest.astype(BF16)
    l = (rest - m.astype(F32)).astype(BF16)
    return h, m, l


def nt(a, b):
    return lax.dot_general(a, b, (((1,), (1,)), ((), ())), preferred_element_type=F32)


def gram_kernel(first, last, merge, base, *refs):
    own, r1, r3, r2, factor_ref = refs[:5]
    refs = refs[5:]
    acc_in = None
    if not first:
        acc_in, core_in = refs[:2]
        refs = refs[2:]
    if last:
        mine_ref, give_ref, core_ref, h_scr, m_scr, l_scr, core_scr, acc_ref = refs
    else:
        acc_ref, core_ref, h_scr, m_scr, l_scr, core_scr = refs
    me = lax.axis_index("narrow")
    step = pl.program_id(0)
    for shift, piece in ((0, own), (1, r1), (3, r3), (2, r2)):
        row = pl.multiple_of(lax.rem(me + 4 - shift, 4) * 128, 128)
        for a in range(own.shape[0]):
            h, m, l = split(piece[a])
            lanes = slice(a * 128, (a + 1) * 128)
            h_scr[pl.ds(row, 128), lanes] = h
            m_scr[pl.ds(row, 128), lanes] = m
            l_scr[pl.ds(row, 128), lanes] = l

    @pl.when(step == 0)
    def _():
        if first:
            acc_ref[...] = jnp.zeros_like(acc_ref)
        else:
            acc_ref[...] = acc_in[...]
        if merge:
            core_scr[:, :64] = core_in[...]

    for top, side in ((256, 0), (512, 256)):
        a = [s[:top, :] for s in (h_scr, m_scr, l_scr)]
        b = [s[side:side + 256, :] for s in (h_scr, m_scr, l_scr)]
        part = nt(a[1], b[1])
        part += nt(a[0], b[2])
        part += nt(a[2], b[0])
        part += nt(a[0], b[1])
        part += nt(a[1], b[0])
        part += nt(a[0], b[0])
        for k, (i, j) in enumerate(BLOCKS):
            if side <= j * 128 < side + 256:
                acc_ref[k * 128:(k + 1) * 128, :] += part[
                    i * 128:(i + 1) * 128, j * 128 - side:j * 128 - side + 128
                ]
    f = jnp.concatenate(split(factor_ref[...]), axis=0)
    by_h = jnp.dot(f, h_scr[...], preferred_element_type=F32)
    by_m = jnp.dot(f[:128], m_scr[...], preferred_element_type=F32)
    by_l = jnp.dot(f[:64], l_scr[...], preferred_element_type=F32)
    core = (by_h[128:] + by_l + by_m[64:]) + (by_h[64:128] + by_m[:64]) + by_h[:64]
    depth = own.shape[0]
    for a in range(depth):
        part = core[:, a * 128:(a + 1) * 128]
        at = base + depth * step + a
        core_scr[pl.ds(at, 64, stride=16), :] = part
        core_scr[pl.ds(at + 8, 64, stride=16), :] = pltpu.roll(part, 64, 1)

    @pl.when(step == pl.num_programs(0) - 1)
    def _():
        core_ref[...] = core_scr[:, :64]
        if last:
            c = lax.axis_index("core")
            mine_ref[...] = acc_ref[pl.ds(pl.multiple_of(c * HALF, 128), HALF), :]
            give_ref[...] = acc_ref[pl.ds(pl.multiple_of((1 - c) * HALF, 128), HALF), :]


def gram_step(comp, base, pieces, factor_t, acc, core, last):
    first = acc is None
    merge = base > 0
    depth = pieces[0].shape[0]
    take = 2 if depth < 4 else depth // 2
    piece_spec = pl.BlockSpec((take, 128, 128), lambda s: (s, 0, 0))
    whole = lambda s: (0, 0)
    in_specs = [piece_spec] * 4 + [pl.BlockSpec((64, 512), whole)]
    core_spec = pl.BlockSpec((None, 1024, 64), lambda s: (comp, 0, 0))
    args = list(pieces) + [factor_t]
    aliases = {}
    if not first:
        in_specs += [
            pl.BlockSpec((1280, 128), whole),
            core_spec if merge else pl.BlockSpec(memory_space=pl.ANY),
        ]
        args += [acc, core]
        aliases = {6: 2} if last else {5: 0, 6: 1}
    sums = [HALF, HALF] if last else [1280]
    scratch = [pltpu.VMEM((512, 128 * take), BF16)] * 3 + [pltpu.VMEM((1024, 128), F32)]
    if last:
        scratch.append(pltpu.VMEM((1280, 128), F32))
    return pl.pallas_call(
        functools.partial(gram_kernel, first, last, merge, base),
        grid=(depth // take,),
        in_specs=in_specs,
        out_specs=[pl.BlockSpec((r, 128), whole) for r in sums] + [core_spec],
        out_shape=[jax.ShapeDtypeStruct((r, 128), F32) for r in sums]
        + [jax.ShapeDtypeStruct((4, 1024, 64), F32)],
        scratch_shapes=scratch,
        input_output_aliases=aliases,
        compiler_params=pltpu.CompilerParams(vmem_limit_bytes=40 << 20),
        cost_estimate=pl.CostEstimate(
            flops=(6 << 26) * depth, bytes_accessed=depth << 19, transcendentals=0
        ),
        name="gram",
    )(*args)


def total(mine, give):
    swap = [(0, 1), (1, 0)]
    plane = lax.axis_size("z") * lax.axis_size("y")
    h = mine + lax.ppermute(give, "core", swap)
    h = h.reshape(plane, HALF // plane, 128)
    deal = lambda x, axes: lax.all_to_all(x, axes, 0, 0, tiled=True)
    spread = lambda x, n: jnp.broadcast_to(x[None], (n,) + x.shape)
    piece = jnp.sum(deal(h, ("z", "y")), axis=0)
    for flip in (1, 3):
        piece += lax.ppermute(piece, "narrow", [(i, i ^ flip) for i in range(4)])
    h = deal(spread(piece, plane), ("z", "y")).reshape(HALF, 128)
    return h, lax.ppermute(h, "core", swap)


def factor_block(work, out_ref, b, tiles):
    lane = lax.broadcasted_iota(jnp.int32, (8, 128), 1)
    sub = lax.broadcasted_iota(jnp.int32, (8, 128), 0)
    base = b * 128
    spread = lambda v, i: jnp.broadcast_to(v[i:i + 1, :], (8, 128))
    column = lambda v, j: jnp.broadcast_to(v[:, j:j + 1], (8, 128))
    for p in range(16):
        at = base + 8 * p
        head = work[b, at:at + 8, :]
        if p % PANEL == 0:
            cols = [column(head, 8 * p + j) for j in range(8)]
        else:
            cols = ncols
        last = p - p % PANEL + PANEL
        more = p + 1 < last
        if more:
            nxt = work[b, at + 8:at + 16, :]
            ncols = [column(nxt, 8 * (p + 1) + j) for j in range(8)]
        c = {(i, j): spread(cols[j], i) for j in range(8) for i in range(j + 1)}
        rs, u = [], {}
        for k in range(8):
            r = lax.rsqrt(c[k, k])
            rs.append(r)
            for j in range(k + 1, 8):
                u[k, j] = c[k, j] * r
            for j in range(k + 1, 8):
                for i in range(k + 1, j + 1):
                    c[i, j] = c[i, j] - u[k, i] * u[k, j]
        rows = {}
        for t in tiles:
            x = head if t == b else work[t, at:at + 8, :]
            made = []
            for k in range(8):
                v = spread(x, k)
                for m in range(k):
                    v = v - u[m, k] * made[m]
                made.append(v * rs[k])
            rows[t] = made
            full = made[0]
            for k in range(1, 8):
                full = jnp.where(sub >= k, made[k], full)
            if t == b:
                full = jnp.where(lane >= sub + 8 * p, full, 0.0)
            out_ref[at:at + 8, t * 128:(t + 1) * 128] = full
        for g in range(p + 1, last):
            ag = base + 8 * g
            a = work[b, ag:ag + 8, :]
            left = [column(a, 8 * p + j) for j in range(8)]
            ug = []
            for k in range(8):
                w = left[k] * rs[k]
                ug.append(w)
                for j in range(k + 1, 8):
                    left[j] = left[j] - w * u[k, j]
                if more and g == p + 1:
                    for j in range(8):
                        ncols[j] = ncols[j] - w * spread(w, j)
            for t in tiles:
                v = a if t == b else work[t, ag:ag + 8, :]
                for k in range(8):
                    v = v - ug[k] * rows[t][k]
                work[t, ag:ag + 8, :] = v
        if p + 1 == last and last < 16:
            done = out_ref[at + 8 - 8 * PANEL:at + 8, base:]
            part = lax.dot_general(
                done[:, :128], done, (((0,), (0,)), ((), ())),
                precision=HI, preferred_element_type=F32,
            )
            for t in tiles:
                o = (t - b) * 128
                work[t, base + 8 * last:base + 128, :] -= part[8 * last:, o:o + 128]


def chol_kernel(scale, mine_ref, other_ref, out_ref, gram, work, sems):
    c = lax.axis_index("core")
    copies = [
        pltpu.make_async_copy(
            ref, gram.at[pl.ds(pl.multiple_of(at * HALF, 128), HALF), :], sems.at[k]
        )
        for k, (ref, at) in enumerate(((mine_ref, c), (other_ref, 1 - c)))
    ]
    for copy in copies:
        copy.start()
    for copy in copies:
        copy.wait()
    for k, (i, j) in enumerate(BLOCKS):
        work[j, i * 128:(i + 1) * 128, :] = gram[k * 128:(k + 1) * 128, :] * scale
    for b in range(4):
        factor_block(work, out_ref, b, range(b, 4))
        for t in range(b):
            out_ref[b * 128:(b + 1) * 128, t * 128:(t + 1) * 128] = jnp.zeros((128, 128), F32)
        if b < 3:
            tail = out_ref[b * 128:(b + 1) * 128, (b + 1) * 128:]
            for i in range(b + 1, 4):
                o = (i - b - 1) * 128
                part = lax.dot_general(
                    tail[:, o:o + 128],
                    tail[:, o:],
                    (((0,), (0,)), ((), ())),
                    precision=HI,
                    preferred_element_type=F32,
                )
                for j in range(i, 4):
                    work[j, i * 128:(i + 1) * 128, :] -= part[:, (j - i) * 128:(j - i + 1) * 128]


def upper_factor(mine, other, scale):
    return pl.pallas_call(
        functools.partial(chol_kernel, scale),
        out_shape=jax.ShapeDtypeStruct((512, 512), F32),
        in_specs=[pl.BlockSpec(memory_space=pl.ANY)] * 2,
        out_specs=pl.BlockSpec((512, 512), lambda: (0, 0)),
        scratch_shapes=[
            pltpu.VMEM((1280, 128), F32),
            pltpu.VMEM((4, 512, 128), F32),
            pltpu.SemaphoreType.DMA((2,)),
        ],
        name="upper_factor",
    )(mine, other)


def on_device(slab, factor):
    count, own, second, third = slab.shape
    ncol_total = count * second * lax.axis_size(WIDE) * third
    flat = slab.reshape(count, own * second, third)
    factor_t = factor.T
    acc = core = None
    chunks = []
    for comp, ranges in PLAN:
        for (base, _), p in zip(ranges, pack(flat, comp, ranges)):
            chunks.append((comp, base, p))
    arrived = []
    for at, (c, base, p) in enumerate(chunks):
        arrived.append([lax.ppermute(p[k], "narrow", ring(4, k)) for k in SHIFTS])
    for at, (c, base, p) in enumerate(chunks):
        last = at == len(chunks) - 1
        made = gram_step(c, base, [p[0]] + arrived[at], factor_t, acc, core, last)
        if last:
            mine, give, core = made
        else:
            acc, core = made
    mine, other = total(mine, give)
    r_factor = upper_factor(mine, other, 1.0 / ncol_total)
    return (r_factor, core.reshape(count, 64, second, 64))


def solution(mesh):
    narrow = mesh.shape["narrow"]
    fine = Mesh(mesh.devices.reshape(4, 4, 2, narrow), WIDE + ("narrow",))
    return jax.shard_map(
        on_device,
        mesh=fine,
        in_specs=(P(None, "narrow", WIDE, None), P()),
        out_specs=(P(), P(None, None, WIDE, "narrow")),
        check_vma=False,
    )
```
